256 devices in a mesh: col: 16 (over z, core), row: 16 (over x, y).
Axes of the slice: x: 4, y: 4, z: 8, core: 2. Of those that a mesh axis runs over, the one named last changes fastest.
Arguments:
- lower_cols: float32 [4096, 2048], P('col', 'row'), may hold values from -6 to 6
- pivot_rows: float32 [8192, 4096], P('row', 'col'), as said below
- pattern: int32 [64, 32], replicated, may hold values 0 or 1
- panel_in: float32 [8192, 2048], P('col', 'row'), may hold values from -6 to 6
- diag_in: float32 [64, 128, 128], P('col'), as said below
Outputs:
- panel: float32 [8192, 2048], P('col', 'row')
- factor: float32 [64, 128, 128], P('col')
The draws below stay inside these ranges and needn't reach their ends.
Inputs may be any that keep to these rules, and one draw needn't show every extreme that they name: diag_in holds symmetric blocks with diagonal entries between 2.5 and 4.5; diag_in[j] - dsum[j] is positive definite. `pivot_rows`: entries of size about (32 * B) ** -0.5.
All inputs are finite; a program needn't handle non-finite values.
Results may differ from the reference program's by a relative error of at most 0.00005.
Values sent between devices are 32-bit elements; how exact they have to be, the bound alone decides.
A program may use at most 128 MiB of HBM per device.

```python
import jax
import jax.numpy as jnp
from jax import lax

B = 128
NK = 32
J = 64
ROWS = 2048


def draw_pivot_rows(key, part):
    scale = (NK * B) ** (-0.5)
    values = jax.random.normal(key, (J * B, NK * B), jnp.float32)
    return values * scale


def draw_diag_in(key, part):
    first = jax.random.fold_in(key, 11)
    second = jax.random.fold_in(key, 23)
    third = jax.random.fold_in(key, 37)
    noise = jax.random.normal(first, (J, B, B), jnp.float32)
    noise = noise * (0.3 / (2.0 * B) ** 0.5)
    sym = noise + jnp.swapaxes(noise, 1, 2)
    signs = (2 * jax.random.randint(third, (J, B), 0, 2) - 1).astype(jnp.float32)
    coupled = 0.3 * signs[:, :, None] * signs[:, None, :]
    lift = 2.7 + jax.random.uniform(second, (J, B, 1), jnp.float32)
    return sym + coupled + lift * jnp.eye(B, dtype=jnp.float32)[None]


def place_ends(values, key, least, top_value):
    longest = values.shape.index(max(values.shape))
    spots = []
    for shift in (0, 1):
        where = [jax.random.randint(jax.random.fold_in(key, axis), (), 0, length) for axis, length in enumerate(values.shape)]
        where[longest] = (where[longest] + shift) % values.shape[longest]
        spots.append(tuple(where))
    return values.at[spots[0]].set(least).at[spots[1]].set(top_value)


def levels(stream_key, shape, cuts, smallest, largest):
    gain = 1.0
    for axis_at, blocks in cuts:
        heights = jax.random.uniform(jax.random.fold_in(jax.random.fold_in(stream_key, 6), axis_at), (blocks,), jnp.float32, smallest / len(cuts), largest / len(cuts))
        gain = gain * jnp.repeat(jnp.exp(heights), shape[axis_at] // blocks).reshape((-1,) + (1,) * (len(shape) - 1 - axis_at))
    return gain


def normal_values(rng, shape, spread, bound, cuts=(), kind=jnp.bfloat16):
    result = jax.random.normal(rng, shape, jnp.float32) * spread
    if len(cuts) > 0:
        result = levels(rng, shape, cuts, -0.22, 0.18) * result
    return jnp.clip(result, min=-bound, max=bound).astype(kind)


def setup_inputs(seed: int = 0) -> dict:
    arg_keys = jax.random.split(jax.random.key(seed), 6)
    lower_cols = normal_values(arg_keys[0], (NK * B, ROWS), 1.0, 6.0, ((0, 16), (1, 16)), jnp.float32)
    pivot_rows = draw_pivot_rows(jax.random.fold_in(arg_keys[5], 71), 0)
    pattern = place_ends((jax.random.randint(arg_keys[2], (J, NK), 0, 2) < 1).astype(jnp.int32), jax.random.fold_in(arg_keys[2], 1), 0, 1)
    panel_in = normal_values(arg_keys[3], (J * B, ROWS), 1.0, 6.0, ((0, 16), (1, 16)), jnp.float32)
    diag_in = draw_diag_in(jax.random.fold_in(arg_keys[5], 71), 0)
    return {"lower_cols": lower_cols, "pivot_rows": pivot_rows, "pattern": pattern, "panel_in": panel_in, "diag_in": diag_in}


def reference(lower_cols, pivot_rows, pattern, panel_in, diag_in):
    mask = jnp.repeat(jnp.repeat(pattern.astype(jnp.float32), B, axis=0), B, axis=1)
    masked = pivot_rows * mask
    update = jnp.dot(masked.astype(jnp.float32), lower_cols.astype(jnp.float32), precision=lax.Precision.HIGHEST, preferred_element_type=jnp.float32)
    blocks = masked.reshape(J, B, NK * B)
    dsum = jnp.einsum('jak,jbk->jab', blocks, blocks, precision=lax.Precision.HIGHEST)
    factor = jnp.linalg.cholesky(diag_in - dsum)
    residue = (panel_in - update).reshape(J, B, ROWS)
    solved = lax.linalg.triangular_solve(factor, residue, left_side=True, lower=True)
    return (solved.reshape(J * B, ROWS), factor)
```

```python
import jax
import jax.numpy as jnp
from jax import lax
from jax.experimental import pallas as pl
from jax.experimental.pallas import tpu as pltpu
from jax.sharding import PartitionSpec as P

B = 128
NR = 4
RB = 64
F32 = jnp.float32
BF16 = jnp.bfloat16
MESH = pl.DeviceIdType.MESH
HIGHEST = lax.Precision.HIGHEST


def split(v):
    hi = v.astype(BF16)
    return hi, (v - hi.astype(F32)).astype(BF16)


def move_kernel(
    pat, piv, low, pan, dia, res_o, sm_o,
    ag, bg, bh, bl, lh, ll, part, sd, su, upd, ds, dsd, dsu, sb,
    a_ss, a_rs, af_ss, b_ss, b_rs, r_ss, rd_rs, ru_rs, d_ss, dd_rs, du_rs,
    s1_ss, s1_rs, s2_ss, s2_rs, y_ss, y_rs,
):
    c_me = lax.axis_index("col")
    r_me = lax.axis_index("row")
    z, h = c_me // 2, c_me % 2
    x, y = r_me // 4, r_me % 4
    oh = 1 - h
    xp, xm, xo = (x + 1) % 4, (x + 3) % 4, (x + 2) % 4
    yp, ym, yo = (y + 1) % 4, (y + 3) % 4, (y + 2) % 4
    zp, zm = (z + 1) % 8, (z + 7) % 8
    yh = y // 2

    def dev(zz, hh, xx, yy):
        return (2 * zz + hh, 4 * xx + yy)

    def rcopy(src, dst, ss, rs, to):
        return pltpu.make_async_remote_copy(
            src_ref=src, dst_ref=dst, send_sem=ss, recv_sem=rs, device_id=to, device_id_type=MESH
        )

    here = dev(z, oh, x, y)

    def arrived(slot, ss, rs):
        rcopy(slot, slot, ss, rs, here).wait_recv()

    peers = [here, dev(zp, h, x, y), dev(zm, h, x, y)]
    for hh in (h, oh):
        peers += [dev(z, hh, xx, y) for xx in (xp, xm, xo)]
        peers += [dev(z, hh, x, yy) for yy in (yp, ym, yo)]
    bar = pltpu.get_barrier_semaphore()
    for p in peers:
        pl.semaphore_signal(bar, inc=1, device_id=p, device_id_type=MESH)
    pl.semaphore_wait(bar, len(peers))

    def rows(hh, i):
        return pl.ds(pl.multiple_of(2 * B * hh + RB * i, RB), RB)

    pending = []

    def go(c):
        c.start()
        pending.append(c)

    for i in range(NR):
        go(rcopy(piv.at[rows(oh, i)], ag.at[i, x, h], a_ss.at[i, 0], a_rs.at[i, 0, h], here))
    go(rcopy(low, bg.at[y, h], b_ss.at[0], b_rs.at[0], here))
    go(rcopy(low, bg.at[y, h], b_ss.at[1], b_rs.at[1], dev(z, h, x, yp)))
    go(rcopy(low, bg.at[y, h], b_ss.at[2], b_rs.at[2], dev(z, h, x, ym)))
    for i in range(NR):
        for n, hh in enumerate((h, oh)):
            src = piv.at[rows(hh, i)]
            go(rcopy(src, ag.at[i, x, h], a_ss.at[i, 1 + 2 * n], a_rs.at[i, 1, h], dev(z, hh, xp, y)))
            go(rcopy(src, ag.at[i, x, h], a_ss.at[i, 2 + 2 * n], a_rs.at[i, 2, h], dev(z, hh, xm, y)))
    for i in range(NR):
        ag[i, x, h] = piv[rows(h, i), :]
    bg[y, h] = low[...]

    def weight(xr, i, kap, kb):
        return pat[4 * (4 * xr + y) + 2 * h + i // 2, 2 * (2 * z + kap) + kb].astype(F32)

    for i in range(NR):
        arrived(ag.at[i, x, oh], a_ss.at[i, 0], a_rs.at[i, 0, oh])
    for t in range(2):
        m = jnp.concatenate(
            [
                jnp.concatenate(
                    [
                        ag[i, x, kap, :, kb * B : (kb + 1) * B] * weight(x, i, kap, kb)
                        for kap in range(2)
                        for kb in range(2)
                    ],
                    axis=1,
                )
                for i in (2 * t, 2 * t + 1)
            ],
            axis=0,
        )
        ds[t] = lax.dot_general(
            m, m, (((1,), (1,)), ((), ())), precision=HIGHEST, preferred_element_type=F32
        )

    d0 = (z - 2 * x - yh + 8) % 8

    def takes_down(d, s):
        return (d <= 3) if s == 0 else (d <= 2)

    def takes_up(d, s):
        return (d >= 6) | (d == 0) if s == 0 else (d >= 5) | (d == 0)

    def gives_down(d, s):
        return (d >= 1) & (d <= 4) if s == 0 else (d >= 1) & (d <= 3)

    def gives_up(d, s):
        return (d >= 5) if s == 0 else (d >= 4)

    def dsum_step(t, u):
        at = pl.ds(RB * u, RB)
        k = 2 * t + u

        @pl.when(takes_down(d0, t))
        def _():
            arrived(dsd.at[t, at], d_ss.at[k], dd_rs.at[k])
            ds[t, at, :] += dsd[t, at, :]

        @pl.when(takes_up(d0, t))
        def _():
            arrived(dsu.at[t, at], d_ss.at[k], du_rs.at[k])
            ds[t, at, :] += dsu[t, at, :]

        @pl.when(gives_down(d0, t))
        def _():
            rcopy(ds.at[t, at], dsd.at[t, at], d_ss.at[k], dd_rs.at[k], dev(zm, h, x, y)).start()

        @pl.when(gives_up(d0, t))
        def _():
            rcopy(ds.at[t, at], dsu.at[t, at], d_ss.at[k], du_rs.at[k], dev(zp, h, x, y)).start()

    def forward_b():
        arrived(bg.at[ym, h], b_ss.at[1], b_rs.at[1])
        go(rcopy(bg.at[ym, h, 0:B], bg.at[ym, h, 0:B], b_ss.at[3], b_rs.at[3], dev(z, h, x, yp)))
        go(rcopy(bg.at[ym, h], bg.at[ym, h], b_ss.at[5], b_rs.at[5], here))
        arrived(bg.at[yp, h], b_ss.at[2], b_rs.at[2])
        go(rcopy(bg.at[yp, h, B:], bg.at[yp, h, B:], b_ss.at[4], b_rs.at[4], dev(z, h, x, ym)))
        go(rcopy(bg.at[yp, h], bg.at[yp, h], b_ss.at[6], b_rs.at[6], here))

    def forward_b2():
        arrived(bg.at[yo, h, 0:B], b_ss.at[3], b_rs.at[3])
        go(rcopy(bg.at[yo, h, 0:B], bg.at[yo, h, 0:B], b_ss.at[7], b_rs.at[7], here))
        arrived(bg.at[yo, h, B:], b_ss.at[4], b_rs.at[4])
        go(rcopy(bg.at[yo, h, B:], bg.at[yo, h, B:], b_ss.at[8], b_rs.at[8], here))

    def build_b():
        arrived(bg.at[y, oh], b_ss.at[0], b_rs.at[0])
        arrived(bg.at[ym, oh], b_ss.at[5], b_rs.at[5])
        arrived(bg.at[yp, oh], b_ss.at[6], b_rs.at[6])
        arrived(bg.at[yo, oh, 0:B], b_ss.at[7], b_rs.at[7])
        arrived(bg.at[yo, oh, B:], b_ss.at[8], b_rs.at[8])
        for yy in range(4):
            for kap in range(2):
                hi, lo = split(bg[yy, kap])
                bh[kap * 256 : kap * 256 + 256, yy * B : yy * B + B] = hi
                bl[kap * 256 : kap * 256 + 256, yy * B : yy * B + B] = lo

    def forward_a(i):
        arrived(ag.at[i, xm, 0], a_ss.at[i, 0], a_rs.at[i, 1, 0])
        go(rcopy(ag.at[i, xm, 0], ag.at[i, xm, 0], af_ss.at[i, 0], a_rs.at[i, 3, 0], dev(z, h, xp, y)))
        arrived(ag.at[i, xp, 1], a_ss.at[i, 0], a_rs.at[i, 2, 1])
        go(rcopy(ag.at[i, xp, 1], ag.at[i, xp, 1], af_ss.at[i, 1], a_rs.at[i, 3, 1], dev(z, h, xm, y)))

    def product(i):
        arrived(ag.at[i, xm, 1], a_ss.at[i, 0], a_rs.at[i, 1, 1])
        arrived(ag.at[i, xp, 0], a_ss.at[i, 0], a_rs.at[i, 2, 0])
        arrived(ag.at[i, xo, 0], a_ss.at[i, 0], a_rs.at[i, 3, 0])
        arrived(ag.at[i, xo, 1], a_ss.at[i, 0], a_rs.at[i, 3, 1])
        for xr in range(4):
            for kap in range(2):
                for kb in range(2):
                    v = ag[i, xr, kap, :, kb * B : (kb + 1) * B] * weight(xr, i, kap, kb)
                    hi, lo = split(v)
                    k = (2 * kap + kb) * B
                    lh[xr * RB : xr * RB + RB, k : k + B] = hi
                    ll[xr * RB : xr * RB + RB, k : k + B] = lo
        p = jnp.dot(lh[...], bh[...], preferred_element_type=F32)
        p += jnp.dot(ll[...], bh[...], preferred_element_type=F32)
        p += jnp.dot(lh[...], bl[...], preferred_element_type=F32)
        for xr in range(4):
            part[i, xr] = p[xr * RB : xr * RB + RB]

    par = (z + yh) % 2
    e = (z - yh + 8) % 8
    offs = [jnp.where(par == 0, ev, od) for ev, od in ((4, 3), (2, 5), (6, 1), (0, 7))]
    blks = [((e - d + 8) // 2) % 4 for d in offs]

    def reduce_step(i, q, s, leaf):
        d, xr = offs[q], blks[q]
        at = pl.ds(256 * s, 256)
        mine = part.at[i, xr, :, at]
        ss = r_ss.at[i, q, s]
        tk_d, tk_u = takes_down(d, s), takes_up(d, s)
        if not leaf:

            @pl.when(tk_d)
            def _():
                arrived(sd.at[i, xr, s], ss, rd_rs.at[i, xr, s])
                part[i, xr, :, at] += sd[i, xr, s]

            @pl.when(tk_u)
            def _():
                arrived(su.at[i, xr, s], ss, ru_rs.at[i, xr, s])
                part[i, xr, :, at] += su[i, xr, s]

        first = jnp.logical_not(tk_d | tk_u)
        turn = first if leaf else jnp.logical_not(first)

        @pl.when(turn & gives_down(d, s))
        def _():
            rcopy(mine, sd.at[i, xr, s], ss, rd_rs.at[i, xr, s], dev(zm, h, x, y)).start()

        @pl.when(turn & gives_up(d, s))
        def _():
            rcopy(mine, su.at[i, xr, s], ss, ru_rs.at[i, xr, s], dev(zp, h, x, y)).start()

    c_to = y % 2
    owner = par == 0

    def leaves(i):
        for q in range(2):
            for s in range(2):
                reduce_step(i, q, s, True)

    def middle(i):
        @pl.when(par == 1)
        def _():
            reduce_step(i, 0, 0, False)
            reduce_step(i, 1, 1, False)

        @pl.when(par == 0)
        def _():
            reduce_step(i, 1, 1, False)
            reduce_step(i, 2, 0, False)
            reduce_step(i, 1, 0, False)
            reduce_step(i, 2, 1, False)

    def finish(i):
        @pl.when(par == 1)
        def _():
            for s in range(2):
                reduce_step(i, 2, s, False)
                reduce_step(i, 3, s, False)

        @pl.when(par == 0)
        def _():
            for s in range(2):
                reduce_step(i, 3, s, False)
                for yy in (2 * s, 2 * s + 1):
                    same = (yy == y) & (h == c_to)
                    src = part.at[i, blks[3], :, pl.ds(B * yy, B)]

                    @pl.when(same)
                    def _():
                        upd[rows(h, i), :] = part[i, blks[3], :, pl.ds(B * yy, B)]

                    @pl.when(jnp.logical_not(same))
                    def _():
                        rcopy(
                            src, upd.at[rows(h, i)], y_ss.at[i, yy], y_rs.at[i, h], dev(z, c_to, x, yy)
                        ).start()

    root = d0 == 0
    relay = owner & (h == c_to)

    def sum_x():
        @pl.when(root)
        def _():
            for t in range(2):
                for n, xx in enumerate((xp, xm, xo)):
                    rcopy(
                        ds.at[t], sb.at[2 * h + t], s1_ss.at[t, n], s1_rs.at[2 * h + t], dev(z, c_to, xx, y)
                    ).start()

                @pl.when(h != c_to)
                def _():
                    rcopy(ds.at[t], sb.at[2 * h + t], s1_ss.at[t, 3], s1_rs.at[2 * h + t], here).start()

                @pl.when(h == c_to)
                def _():
                    sb[2 * h + t] = ds[t]

    def sum_y():
        @pl.when(relay)
        def _():
            for t in range(4):
                @pl.when(jnp.logical_not(root & (h == t // 2)))
                def _():
                    arrived(sb.at[t], s1_ss.at[0, 0], s1_rs.at[t])

                for n, yy in enumerate((yp, ym, yo)):
                    rcopy(sb.at[t], sb.at[t], s2_ss.at[t, n], s2_rs.at[t], dev(z, h, x, yy)).start()

    forward_b()
    for t in range(2):
        for u in range(2):
            dsum_step(t, u)
    forward_a(0)
    forward_b2()
    sum_x()
    build_b()
    for i in range(NR):
        product(i)
        leaves(i)
        if i + 1 < NR:
            forward_a(i + 1)
        if i == 1:
            sum_y()
        if i > 0:
            finish(i - 1)
        middle(i)
    finish(NR - 1)

    @pl.when(jnp.logical_not(relay))
    def _():
        for t in range(4):
            arrived(sb.at[t], s2_ss.at[t, 0], s2_rs.at[t])

    sm_o[...] = dia[...] - sb[...]
    y_src = 2 * (z % 2) + h
    for i in range(NR):
        for hh in range(2):

            @pl.when(jnp.logical_not((y == y_src) & (h == hh)))
            def _():
                arrived(upd.at[rows(hh, i)], y_ss.at[i, 0], y_rs.at[i, hh])

            res_o[rows(hh, i), :] = pan[rows(hh, i), :] - upd[rows(hh, i), :]

    for c in pending:
        c.wait_send()
    for t in range(2):
        for u in range(2):
            k = 2 * t + u
            at = pl.ds(RB * u, RB)

            @pl.when(jnp.logical_not(root))
            def _():
                rcopy(ds.at[t, at], dsd.at[t, at], d_ss.at[k], dd_rs.at[k], here).wait_send()

    for i in range(NR):
        for q in range(4):
            for s in range(2):

                @pl.when(offs[q] != 0)
                def _():
                    rcopy(
                        part.at[i, blks[q], :, pl.ds(256 * s, 256)], sd.at[i, blks[q], s],
                        r_ss.at[i, q, s], rd_rs.at[i, blks[q], s], here,
                    ).wait_send()

        @pl.when(owner)
        def _():
            for yy in range(4):
                @pl.when(jnp.logical_not((yy == y) & (h == c_to)))
                def _():
                    rcopy(
                        part.at[i, blks[3], :, pl.ds(B * yy, B)], upd.at[rows(h, i)],
                        y_ss.at[i, yy], y_rs.at[i, h], here,
                    ).wait_send()

    @pl.when(root)
    def _():
        for t in range(2):
            for n in range(3):
                rcopy(ds.at[t], sb.at[t], s1_ss.at[t, n], s1_rs.at[t], here).wait_send()

            @pl.when(h != c_to)
            def _():
                rcopy(ds.at[t], sb.at[t], s1_ss.at[t, 3], s1_rs.at[t], here).wait_send()

    @pl.when(relay)
    def _():
        for t in range(4):
            for n in range(3):
                rcopy(sb.at[t], sb.at[t], s2_ss.at[t, n], s2_rs.at[t], here).wait_send()


def move(pattern, pivot_rows, lower_cols, panel_in, diag_in):
    vm = pl.BlockSpec(memory_space=pltpu.VMEM)
    dma = pltpu.SemaphoreType.DMA
    return pl.pallas_call(
        move_kernel,
        out_shape=(
            jax.ShapeDtypeStruct((4 * B, B), F32),
            jax.ShapeDtypeStruct((4, B, B), F32),
        ),
        in_specs=[pl.BlockSpec(memory_space=pltpu.SMEM)] + [vm] * 4,
        out_specs=(vm, vm),
        scratch_shapes=[
            pltpu.VMEM((NR, 4, 2, RB, 256), F32),
            pltpu.VMEM((4, 2, 256, B), F32),
            pltpu.VMEM((512, 512), BF16),
            pltpu.VMEM((512, 512), BF16),
            pltpu.VMEM((256, 512), BF16),
            pltpu.VMEM((256, 512), BF16),
            pltpu.VMEM((NR, 4, RB, 512), F32),
            pltpu.VMEM((NR, 4, 2, RB, 256), F32),
            pltpu.VMEM((NR, 4, 2, RB, 256), F32),
            pltpu.VMEM((4 * B, B), F32),
            pltpu.VMEM((2, B, B), F32),
            pltpu.VMEM((2, B, B), F32),
            pltpu.VMEM((2, B, B), F32),
            pltpu.VMEM((4, B, B), F32),
            dma((NR, 5)), dma((NR, 4, 2)), dma((NR, 2)), dma((9,)), dma((9,)),
            dma((NR, 4, 2)), dma((NR, 4, 2)), dma((NR, 4, 2)), dma((4,)), dma((4,)), dma((4,)),
            dma((2, 4)), dma((4,)), dma((4, 3)), dma((4,)), dma((NR, 4)), dma((NR, 2)),
        ],
        compiler_params=pltpu.CompilerParams(
            collective_id=0, has_side_effects=True, vmem_limit_bytes=48 << 20
        ),
        name="move",
    )(pattern, pivot_rows, lower_cols, panel_in, diag_in)


PB = 32


def factor_kernel(sm, res, out, fac, am, mi):
    row8 = lax.broadcasted_iota(jnp.int32, (8, B), 0)
    lane8 = lax.broadcasted_iota(jnp.int32, (8, B), 1)
    am[...] = sm[...]
    eye = (
        lax.broadcasted_iota(jnp.int32, (B, B), 0) == lax.broadcasted_iota(jnp.int32, (B, B), 1)
    ).astype(F32)
    for m in range(4):
        mi[m] = eye
    nv = PB // 8
    for b in range(B // PB):
        lo = PB * b
        ra = [[am[m, lo + 8 * v : lo + 8 * v + 8, :] for v in range(nv)] for m in range(4)]
        rm = [[mi[m, lo + 8 * v : lo + 8 * v + 8, :] for v in range(nv)] for m in range(4)]
        for i in range(PB):
            v0, s0 = i // 8, i % 8
            j = lo + i
            for m in range(4):
                row = ra[m][v0][s0 : s0 + 1, :]
                mrow = rm[m][v0][s0 : s0 + 1, :]
                cols = [
                    jnp.broadcast_to(ra[m][v][:, j : j + 1], (8, B)) if v >= v0 else None
                    for v in range(nv)
                ]
                inv = 1.0 / cols[v0][s0 : s0 + 1, :]
                row, mrow = row * inv, mrow * inv
                for v in range(v0, nv):
                    f = cols[v]
                    if v == v0:
                        if s0 == 7:
                            continue
                        f = jnp.where(row8 > s0, f, 0.0)
                    ra[m][v] = ra[m][v] - f * row
                    rm[m][v] = rm[m][v] - f * mrow
        for m in range(4):
            ls, ms = [], []
            for v in range(nv):
                on = lane8 - row8 - (lo + 8 * v)
                d = jnp.sum(jnp.where(on == 0, ra[m][v], 0.0), axis=1, keepdims=True)
                s = lax.rsqrt(d)
                s = s * (1.5 - 0.5 * d * s * s)
                ls.append(jnp.where(on >= 0, ra[m][v] * s, 0.0))
                ms.append(rm[m][v] * s)
            ls = jnp.concatenate(ls, axis=0)
            ms = jnp.concatenate(ms, axis=0)
            mi[m, lo : lo + PB, :] = ms
            lt = ls.T
            fac[m, :, lo : lo + PB] = lt
            if lo + PB < B:
                g = jnp.dot(
                    lt[lo + PB :, :],
                    jnp.concatenate([ls, ms], axis=1),
                    precision=HIGHEST,
                    preferred_element_type=F32,
                )
                am[m, lo + PB :, :] -= g[:, :B]
                mi[m, lo + PB :, :] -= g[:, B:]
    for m in range(4):
        out[m * B : m * B + B, :] = jnp.dot(
            mi[m], res[m * B : m * B + B, :], precision=HIGHEST, preferred_element_type=F32
        )


def factor_solve(sm, res):
    vm = pl.BlockSpec(memory_space=pltpu.VMEM)
    return pl.pallas_call(
        factor_kernel,
        out_shape=(
            jax.ShapeDtypeStruct((4 * B, B), F32),
            jax.ShapeDtypeStruct((4, B, B), F32),
        ),
        in_specs=[vm, vm],
        out_specs=(vm, vm),
        scratch_shapes=[pltpu.VMEM((4, B, B), F32), pltpu.VMEM((4, B, B), F32)],
        name="factor_solve",
    )(sm, res)


def shards(lower_cols, pivot_rows, pattern, panel_in, diag_in):
    res, sm = move(pattern, pivot_rows, lower_cols, panel_in, diag_in)
    return factor_solve(sm, res)


def solution(mesh):
    in_specs = (P("col", "row"), P("row", "col"), P(), P("col", "row"), P("col", None, None))
    out_specs = (P("col", "row"), P("col", None, None))
    return jax.shard_map(shards, mesh=mesh, in_specs=in_specs, out_specs=out_specs, check_vma=False)
```

```python
import jax
import jax.numpy as jnp
from jax import lax
from jax.experimental import pallas as pl
from jax.experimental.pallas import tpu as pltpu
from jax.sharding import PartitionSpec as P

B = 128
NR = 4
RB = 64
F32 = jnp.float32
BF16 = jnp.bfloat16
MESH = pl.DeviceIdType.MESH
HIGHEST = lax.Precision.HIGHEST


def split(v):
    hi = v.astype(BF16)
    return hi, (v - hi.astype(F32)).astype(BF16)


PB = 32


def factor_panel(b, am, mi, fac):
    row8 = lax.broadcasted_iota(jnp.int32, (8, B), 0)
    lane8 = lax.broadcasted_iota(jnp.int32, (8, B), 1)
    nv = PB // 8
    lo = PB * b
    ra = [[am[m, lo + 8 * v : lo + 8 * v + 8, :] for v in range(nv)] for m in range(4)]
    rm = [[mi[m, lo + 8 * v : lo + 8 * v + 8, :] for v in range(nv)] for m in range(4)]
    for v0 in range(nv):
        at = lo + 8 * v0
        cols = [
            [
                [jnp.broadcast_to(ra[m][v][:, at + k : at + k + 1], (8, B)) for v in range(v0, nv)]
                for k in range(8)
            ]
            for m in range(4)
        ]
        for k in range(8):
            for m in range(4):
                c = cols[m]
                inv = 1.0 / c[k][0][k : k + 1, :]
                row = ra[m][v0][k : k + 1, :] * inv
                mrow = rm[m][v0][k : k + 1, :] * inv
                scal = [c[kk][0][k : k + 1, :] * inv for kk in range(k + 1, 8)]
                for v in range(v0, nv):
                    f = c[k][v - v0]
                    if v == v0:
                        if k == 7:
                            continue
                        f = jnp.where(row8 > k, f, 0.0)
                    for kk in range(k + 1, 8):
                        c[kk][v - v0] = c[kk][v - v0] - f * scal[kk - k - 1]
                    ra[m][v] = ra[m][v] - f * row
                    rm[m][v] = rm[m][v] - f * mrow
    for m in range(4):
        ls, ms = [], []
        for v in range(nv):
            on = lane8 - row8 - (lo + 8 * v)
            d = jnp.sum(jnp.where(on == 0, ra[m][v], 0.0), axis=1, keepdims=True)
            s = lax.rsqrt(d)
            s = s * (1.5 - 0.5 * d * s * s)
            ls.append(jnp.where(on >= 0, ra[m][v] * s, 0.0))
            ms.append(rm[m][v] * s)
        ls = jnp.concatenate(ls, axis=0)
        ms = jnp.concatenate(ms, axis=0)
        mi[m, lo : lo + PB, :] = ms
        lt = ls.T
        fac[m, :, lo : lo + PB] = lt
        if lo + PB < B:
            g = jnp.dot(
                lt[lo + PB :, :],
                jnp.concatenate([ls, ms], axis=1),
                precision=HIGHEST,
                preferred_element_type=F32,
            )
            am[m, lo + PB :, :] -= g[:, :B]
            mi[m, lo + PB :, :] -= g[:, B:]


def window_kernel(
    pat_h, piv, low, pan_h, dia_h, out_h, fac_h,
    pat, ag, bg, bh, bl, lh, ll, part, sd, su, upd, ds, dsd, dsu, sb, pan, am, mi, fac, out,
    l_ss, a_ss, a_rs, af_ss, b_ss, b_rs, r_ss, rd_rs, ru_rs, d_ss, dd_rs, du_rs,
    s1_ss, s1_rs, s2_ss, s2_rs, y_ss, y_rs,
):
    c_me = lax.axis_index("col")
    r_me = lax.axis_index("row")
    z, h = c_me // 2, c_me % 2
    x, y = r_me // 4, r_me % 4
    oh = 1 - h
    xp, xm, xo = (x + 1) % 4, (x + 3) % 4, (x + 2) % 4
    yp, ym, yo = (y + 1) % 4, (y + 3) % 4, (y + 2) % 4
    zp, zm = (z + 1) % 8, (z + 7) % 8
    yh = y // 2

    own = [
        pltpu.make_async_copy(piv.at[pl.ds(NR * h, NR)], ag.at[:, x, h], l_ss.at[0]),
        pltpu.make_async_copy(pat_h, pat, l_ss.at[1]),
        pltpu.make_async_copy(low, bg.at[y, h], l_ss.at[2]),
        pltpu.make_async_copy(dia_h, am, l_ss.at[3]),
        pltpu.make_async_copy(pan_h, pan, l_ss.at[4]),
    ]
    for c in own:
        c.start()

    def dev(zz, hh, xx, yy):
        return (2 * zz + hh, 4 * xx + yy)

    def rcopy(src, dst, ss, rs, to):
        return pltpu.make_async_remote_copy(
            src_ref=src, dst_ref=dst, send_sem=ss, recv_sem=rs, device_id=to, device_id_type=MESH
        )

    here = dev(z, oh, x, y)

    def arrived(slot, ss, rs):
        rcopy(slot, slot, ss, rs, here).wait_recv()

    peers = [here, dev(zp, h, x, y), dev(zm, h, x, y)]
    for hh in (h, oh):
        peers += [dev(z, hh, xx, y) for xx in (xp, xm, xo)]
        peers += [dev(z, hh, x, yy) for yy in (yp, ym, yo)]
    bar = pltpu.get_barrier_semaphore()
    for p in peers:
        pl.semaphore_signal(bar, inc=1, device_id=p, device_id_type=MESH)
    pl.semaphore_wait(bar, len(peers))

    def rows(hh, i):
        return pl.ds(pl.multiple_of(2 * B * hh + RB * i, RB), RB)

    pending = []

    def go(c):
        c.start()
        pending.append(c)

    def send_a(i):
        for n, hh in enumerate((h, oh)):
            src = piv.at[NR * hh + i]
            go(rcopy(src, ag.at[i, x, h], a_ss.at[i, 2 * n], a_rs.at[i, 1, h], dev(z, hh, xp, y)))
            go(rcopy(src, ag.at[i, x, h], a_ss.at[i, 1 + 2 * n], a_rs.at[i, 2, h], dev(z, hh, xm, y)))

    go(rcopy(piv.at[pl.ds(NR * oh, NR)], ag.at[:, x, h], b_ss.at[9], b_rs.at[9], here))
    go(rcopy(low, bg.at[y, h], b_ss.at[1], b_rs.at[1], dev(z, h, x, yp)))
    go(rcopy(low, bg.at[y, h], b_ss.at[2], b_rs.at[2], dev(z, h, x, ym)))
    send_a(0)
    go(rcopy(low, bg.at[y, h], b_ss.at[0], b_rs.at[0], here))

    def weight(xr, i, kap, kb):
        return pat[4 * (4 * xr + y) + 2 * h + i // 2, 2 * (2 * z + kap) + kb].astype(F32)

    own[0].wait()
    own[1].wait()
    arrived(ag.at[:, x, oh], b_ss.at[9], b_rs.at[9])
    for t in range(2):
        m = jnp.concatenate(
            [
                jnp.concatenate(
                    [
                        ag[i, x, kap, :, kb * B : (kb + 1) * B] * weight(x, i, kap, kb)
                        for kap in range(2)
                        for kb in range(2)
                    ],
                    axis=1,
                )
                for i in (2 * t, 2 * t + 1)
            ],
            axis=0,
        )
        ds[t] = lax.dot_general(
            m, m, (((1,), (1,)), ((), ())), precision=HIGHEST, preferred_element_type=F32
        )

    d0 = (z - 2 * x - yh + 8) % 8

    def takes_down(d, s):
        return (d <= 3) if s == 0 else (d <= 2)

    def takes_up(d, s):
        return (d >= 6) | (d == 0) if s == 0 else (d >= 5) | (d == 0)

    def gives_down(d, s):
        return (d >= 1) & (d <= 4) if s == 0 else (d >= 1) & (d <= 3)

    def gives_up(d, s):
        return (d >= 5) if s == 0 else (d >= 4)

    def dsum_step(t, u, leaf):
        at = pl.ds(RB * u, RB)
        k = 2 * t + u
        tk_d, tk_u = takes_down(d0, t), takes_up(d0, t)
        if not leaf:

            @pl.when(tk_d)
            def _():
                arrived(dsd.at[t, at], d_ss.at[k], dd_rs.at[k])
                ds[t, at, :] += dsd[t, at, :]

            @pl.when(tk_u)
            def _():
                arrived(dsu.at[t, at], d_ss.at[k], du_rs.at[k])
                ds[t, at, :] += dsu[t, at, :]

        first = jnp.logical_not(tk_d | tk_u)
        turn = first if leaf else jnp.logical_not(first)

        @pl.when(turn & gives_down(d0, t))
        def _():
            rcopy(ds.at[t, at], dsd.at[t, at], d_ss.at[k], dd_rs.at[k], dev(zm, h, x, y)).start()

        @pl.when(turn & gives_up(d0, t))
        def _():
            rcopy(ds.at[t, at], dsu.at[t, at], d_ss.at[k], du_rs.at[k], dev(zp, h, x, y)).start()

    def forward_b():
        arrived(bg.at[ym, h], b_ss.at[1], b_rs.at[1])
        go(rcopy(bg.at[ym, h, 0:B], bg.at[ym, h, 0:B], b_ss.at[3], b_rs.at[3], dev(z, h, x, yp)))
        go(rcopy(bg.at[ym, h], bg.at[ym, h], b_ss.at[5], b_rs.at[5], here))
        arrived(bg.at[yp, h], b_ss.at[2], b_rs.at[2])
        go(rcopy(bg.at[yp, h, B:], bg.at[yp, h, B:], b_ss.at[4], b_rs.at[4], dev(z, h, x, ym)))
        go(rcopy(bg.at[yp, h], bg.at[yp, h], b_ss.at[6], b_rs.at[6], here))

    def far_b():
        return (
            rcopy(bg.at[yo, h, 0:B], bg.at[yo, h, 0:B], b_ss.at[7], b_rs.at[7], here),
            rcopy(bg.at[yo, h, B:], bg.at[yo, h, B:], b_ss.at[8], b_rs.at[8], here),
        )

    def forward_b2():
        lower, upper = far_b()
        arrived(bg.at[yo, h, 0:B], b_ss.at[3], b_rs.at[3])
        lower.start()
        arrived(bg.at[yo, h, B:], b_ss.at[4], b_rs.at[4])
        upper.start()

    def build_b():
        own[2].wait()
        arrived(bg.at[y, oh], b_ss.at[0], b_rs.at[0])
        arrived(bg.at[ym, oh], b_ss.at[5], b_rs.at[5])
        arrived(bg.at[yp, oh], b_ss.at[6], b_rs.at[6])
        arrived(bg.at[yo, oh, 0:B], b_ss.at[7], b_rs.at[7])
        arrived(bg.at[yo, oh, B:], b_ss.at[8], b_rs.at[8])
        for yy in range(4):
            for kap in range(2):
                hi, lo = split(bg[yy, kap])
                bh[kap * 256 : kap * 256 + 256, yy * B : yy * B + B] = hi
                bl[kap * 256 : kap * 256 + 256, yy * B : yy * B + B] = lo

    def forward_a(i):
        arrived(ag.at[i, xm, 0], a_ss.at[i, 0], a_rs.at[i, 1, 0])
        go(rcopy(ag.at[i, xm, 0], ag.at[i, xm, 0], af_ss.at[i, 0], a_rs.at[i, 3, 0], dev(z, h, xp, y)))
        arrived(ag.at[i, xp, 1], a_ss.at[i, 0], a_rs.at[i, 2, 1])
        go(rcopy(ag.at[i, xp, 1], ag.at[i, xp, 1], af_ss.at[i, 1], a_rs.at[i, 3, 1], dev(z, h, xm, y)))

    def product(i):
        arrived(ag.at[i, xm, 1], a_ss.at[i, 0], a_rs.at[i, 1, 1])
        arrived(ag.at[i, xp, 0], a_ss.at[i, 0], a_rs.at[i, 2, 0])
        arrived(ag.at[i, xo, 0], a_ss.at[i, 0], a_rs.at[i, 3, 0])
        arrived(ag.at[i, xo, 1], a_ss.at[i, 0], a_rs.at[i, 3, 1])
        for xr in range(4):
            for kap in range(2):
                for kb in range(2):
                    v = ag[i, xr, kap, :, kb * B : (kb + 1) * B] * weight(xr, i, kap, kb)
                    hi, lo = split(v)
                    k = (2 * kap + kb) * B
                    lh[xr * RB : xr * RB + RB, k : k + B] = hi
                    ll[xr * RB : xr * RB + RB, k : k + B] = lo
        p = jnp.dot(lh[...], bh[...], preferred_element_type=F32)
        p += jnp.dot(ll[...], bh[...], preferred_element_type=F32)
        p += jnp.dot(lh[...], bl[...], preferred_element_type=F32)
        for xr in range(4):
            part[i, xr] = p[xr * RB : xr * RB + RB]

    par = (z + yh) % 2
    odd, even = par == 1, par == 0
    e = (z - yh + 8) % 8
    offs = [jnp.where(even, ev, od) for ev, od in ((4, 3), (2, 5), (6, 1), (0, 7))]
    blks = [((e - d + 8) // 2) % 4 for d in offs]

    def reduce_step(i, q, s, leaf):
        d, xr = offs[q], blks[q]
        at = pl.ds(256 * s, 256)
        mine = part.at[i, xr, :, at]
        ss = r_ss.at[i, q, s]
        tk_d, tk_u = takes_down(d, s), takes_up(d, s)
        if not leaf:

            @pl.when(tk_d)
            def _():
                arrived(sd.at[i, xr, s], ss, rd_rs.at[i, xr, s])
                part[i, xr, :, at] += sd[i, xr, s]

            @pl.when(tk_u)
            def _():
                arrived(su.at[i, xr, s], ss, ru_rs.at[i, xr, s])
                part[i, xr, :, at] += su[i, xr, s]

        first = jnp.logical_not(tk_d | tk_u)
        turn = first if leaf else jnp.logical_not(first)

        @pl.when(turn & gives_down(d, s))
        def _():
            rcopy(mine, sd.at[i, xr, s], ss, rd_rs.at[i, xr, s], dev(zm, h, x, y)).start()

        @pl.when(turn & gives_up(d, s))
        def _():
            rcopy(mine, su.at[i, xr, s], ss, ru_rs.at[i, xr, s], dev(zp, h, x, y)).start()

    c_to = y % 2

    def leaves(i):
        for q in range(2):
            for s in range(2):
                reduce_step(i, q, s, True)

    def stage1(i):
        reduce_step(i, 0, 0, False)
        reduce_step(i, 1, 1, False)

    def stage2(i):
        reduce_step(i, 1, 1, False)
        reduce_step(i, 2, 0, False)
        reduce_step(i, 1, 0, False)
        reduce_step(i, 2, 1, False)

    def stage3(i):
        reduce_step(i, 2, 1, False)
        reduce_step(i, 3, 0, False)
        reduce_step(i, 2, 0, False)
        reduce_step(i, 3, 1, False)

    def stage4(i):
        for s in range(2):
            reduce_step(i, 3, s, False)
            for yy in (2 * s, 2 * s + 1):
                same = (yy == y) & (h == c_to)
                src = part.at[i, blks[3], :, pl.ds(B * yy, B)]

                @pl.when(same)
                def _():
                    upd[rows(h, i), :] = part[i, blks[3], :, pl.ds(B * yy, B)]

                @pl.when(jnp.logical_not(same))
                def _():
                    rcopy(
                        src, upd.at[rows(h, i)], y_ss.at[i, yy], y_rs.at[i, h], dev(z, c_to, x, yy)
                    ).start()

    root = d0 == 0
    relay = even & (h == c_to)

    def sum_x():
        @pl.when(root)
        def _():
            for t in range(2):
                for n, xx in enumerate((xp, xm, xo)):
                    rcopy(
                        ds.at[t], sb.at[2 * h + t], s1_ss.at[t, n], s1_rs.at[2 * h + t], dev(z, c_to, xx, y)
                    ).start()

                @pl.when(h != c_to)
                def _():
                    rcopy(ds.at[t], sb.at[2 * h + t], s1_ss.at[t, 3], s1_rs.at[2 * h + t], here).start()

                @pl.when(h == c_to)
                def _():
                    sb[2 * h + t] = ds[t]

    def sum_y():
        @pl.when(relay)
        def _():
            for t in range(4):
                @pl.when(jnp.logical_not(root & (h == t // 2)))
                def _():
                    arrived(sb.at[t], s1_ss.at[0, 0], s1_rs.at[t])

                for n, yy in enumerate((yp, ym, yo)):
                    rcopy(sb.at[t], sb.at[t], s2_ss.at[t, n], s2_rs.at[t], dev(z, h, x, yy)).start()

    def start_factor():
        own[3].wait()

        @pl.when(jnp.logical_not(relay))
        def _():
            for t in range(4):
                arrived(sb.at[t], s2_ss.at[t, 0], s2_rs.at[t])

        am[...] = am[...] - sb[...]
        eye = (
            lax.broadcasted_iota(jnp.int32, (B, B), 0) == lax.broadcasted_iota(jnp.int32, (B, B), 1)
        ).astype(F32)
        for m in range(4):
            mi[m] = eye

    near = (d0 <= 1) | (d0 == 7)
    pieces = [(t, u) for t in range(2) for u in range(2)]
    for t, u in pieces:
        dsum_step(t, u, True)
    forward_a(0)
    send_a(1)
    forward_b()
    pl.when(near)(forward_b2)
    for t, u in pieces:
        dsum_step(t, u, False)
    sum_x()
    pl.when(jnp.logical_not(near))(forward_b2)
    pending.extend(far_b())
    build_b()

    def on_odd(*steps):
        @pl.when(odd)
        def _():
            for f, i in steps:
                f(i)

    def on_even(*steps):
        @pl.when(even)
        def _():
            for f, i in steps:
                f(i)

    for i in range(NR):
        product(i)
        leaves(i)
        if i + 1 < NR:
            forward_a(i + 1)
        if i + 2 < NR:
            send_a(i + 2)
        if i == 2:
            sum_y()
        on_odd(*([(stage1, i)] + ([(stage3, i - 2)] if i >= 2 else [])))
        on_even(*(([(stage2, i - 1)] if i >= 1 else []) + ([(stage4, i - 3)] if i >= 3 else [])))
    start_factor()
    factor_panel(0, am, mi, fac)
    on_odd((stage3, 2))
    on_even((stage2, 3), (stage4, 1))
    factor_panel(1, am, mi, fac)
    on_odd((stage3, 3))
    on_even((stage4, 2))
    factor_panel(2, am, mi, fac)
    on_even((stage4, 3))
    factor_panel(3, am, mi, fac)
    fac_out = pltpu.make_async_copy(fac, fac_h, l_ss.at[5])
    fac_out.start()

    own[4].wait()
    y_src = 2 * (z % 2) + h
    for i in range(NR):
        for hh in range(2):

            @pl.when(jnp.logical_not((y == y_src) & (h == hh)))
            def _():
                arrived(upd.at[rows(hh, i)], y_ss.at[i, 0], y_rs.at[i, hh])

    for m in range(4):
        at = slice(m * B, m * B + B)
        out[at, :] = jnp.dot(
            mi[m], pan[at, :] - upd[at, :], precision=HIGHEST, preferred_element_type=F32
        )
    panel_out = pltpu.make_async_copy(out, out_h, l_ss.at[6])
    panel_out.start()

    for c in pending:
        c.wait_send()
    for t, u in pieces:
        k = 2 * t + u
        at = pl.ds(RB * u, RB)

        @pl.when(jnp.logical_not(root))
        def _():
            rcopy(ds.at[t, at], dsd.at[t, at], d_ss.at[k], dd_rs.at[k], here).wait_send()

    for i in range(NR):
        for q in range(4):
            for s in range(2):

                @pl.when(offs[q] != 0)
                def _():
                    rcopy(
                        part.at[i, blks[q], :, pl.ds(256 * s, 256)], sd.at[i, blks[q], s],
                        r_ss.at[i, q, s], rd_rs.at[i, blks[q], s], here,
                    ).wait_send()

        @pl.when(even)
        def _():
            for yy in range(4):
                @pl.when(jnp.logical_not((yy == y) & (h == c_to)))
                def _():
                    rcopy(
                        part.at[i, blks[3], :, pl.ds(B * yy, B)], upd.at[rows(h, i)],
                        y_ss.at[i, yy], y_rs.at[i, h], here,
                    ).wait_send()

    @pl.when(root)
    def _():
        for t in range(2):
            for n in range(3):
                rcopy(ds.at[t], sb.at[t], s1_ss.at[t, n], s1_rs.at[t], here).wait_send()

            @pl.when(h != c_to)
            def _():
                rcopy(ds.at[t], sb.at[t], s1_ss.at[t, 3], s1_rs.at[t], here).wait_send()

    @pl.when(relay)
    def _():
        for t in range(4):
            for n in range(3):
                rcopy(sb.at[t], sb.at[t], s2_ss.at[t, n], s2_rs.at[t], here).wait_send()

    fac_out.wait()
    panel_out.wait()


def window(pattern, pivot_rows, lower_cols, panel_in, diag_in):
    anyspace = pl.BlockSpec(memory_space=pltpu.HBM)
    dma = pltpu.SemaphoreType.DMA
    return pl.pallas_call(
        window_kernel,
        out_shape=(
            jax.ShapeDtypeStruct((4 * B, B), F32),
            jax.ShapeDtypeStruct((4, B, B), F32),
        ),
        in_specs=[anyspace] * 5,
        out_specs=(anyspace, anyspace),
        scratch_shapes=[
            pltpu.SMEM((64, 32), jnp.int32),
            pltpu.VMEM((NR, 4, 2, RB, 256), F32),
            pltpu.VMEM((4, 2, 256, B), F32),
            pltpu.VMEM((512, 512), BF16),
            pltpu.VMEM((512, 512), BF16),
            pltpu.VMEM((4 * RB, 512), BF16),
            pltpu.VMEM((4 * RB, 512), BF16),
            pltpu.VMEM((NR, 4, RB, 512), F32),
            pltpu.VMEM((NR, 4, 2, RB, 256), F32),
            pltpu.VMEM((NR, 4, 2, RB, 256), F32),
            pltpu.VMEM((4 * B, B), F32),
            pltpu.VMEM((2, B, B), F32),
            pltpu.VMEM((2, B, B), F32),
            pltpu.VMEM((2, B, B), F32),
            pltpu.VMEM((4, B, B), F32),
            pltpu.VMEM((4 * B, B), F32),
            pltpu.VMEM((4, B, B), F32),
            pltpu.VMEM((4, B, B), F32),
            pltpu.VMEM((4, B, B), F32),
            pltpu.VMEM((4 * B, B), F32),
            dma((7,)), dma((NR, 4)), dma((NR, 4, 2)), dma((NR, 2)), dma((10,)), dma((10,)),
            dma((NR, 4, 2)), dma((NR, 4, 2)), dma((NR, 4, 2)), dma((4,)), dma((4,)), dma((4,)),
            dma((2, 4)), dma((4,)), dma((4, 3)), dma((4,)), dma((NR, 4)), dma((NR, 2)),
        ],
        compiler_params=pltpu.CompilerParams(
            collective_id=0, has_side_effects=True, vmem_limit_bytes=60 << 20
        ),
        name="window",
    )(pattern, pivot_rows.reshape(2 * NR, RB, 256), lower_cols, panel_in, diag_in)


def shards(lower_cols, pivot_rows, pattern, panel_in, diag_in):
    return window(pattern, pivot_rows, lower_cols, panel_in, diag_in)


def solution(mesh):
    in_specs = (P("col", "row"), P("row", "col"), P(), P("col", "row"), P("col", None, None))
    out_specs = (P("col", "row"), P("col", None, None))
    return jax.shard_map(shards, mesh=mesh, in_specs=in_specs, out_specs=out_specs, check_vma=False)
```

```python
import jax
import jax.numpy as jnp
from jax import lax
from jax.experimental import pallas as pl
from jax.experimental.pallas import tpu as pltpu
from jax.sharding import PartitionSpec as P

B = 128
NR = 4
RB = 64
F32 = jnp.float32
BF16 = jnp.bfloat16
MESH = pl.DeviceIdType.MESH
HIGHEST = lax.Precision.HIGHEST


def split(v):
    hi = v.astype(BF16)
    return hi, (v - hi.astype(F32)).astype(BF16)


PB = 32


def factor_panel(b, am, mi, fac):
    row8 = lax.broadcasted_iota(jnp.int32, (8, B), 0)
    lane8 = lax.broadcasted_iota(jnp.int32, (8, B), 1)
    nv = PB // 8
    lo = PB * b
    ra = [[am[m, lo + 8 * v : lo + 8 * v + 8, :] for v in range(nv)] for m in range(4)]
    rm = [[mi[m, lo + 8 * v : lo + 8 * v + 8, :] for v in range(nv)] for m in range(4)]
    for v0 in range(nv):
        at = lo + 8 * v0
        cols = [
            [
                [jnp.broadcast_to(ra[m][v][:, at + k : at + k + 1], (8, B)) for v in range(v0, nv)]
                for k in range(8)
            ]
            for m in range(4)
        ]
        for k in range(8):
            for m in range(4):
                c = cols[m]
                inv = 1.0 / c[k][0][k : k + 1, :]
                row = ra[m][v0][k : k + 1, :] * inv
                mrow = rm[m][v0][k : k + 1, :] * inv
                scal = [c[kk][0][k : k + 1, :] * inv for kk in range(k + 1, 8)]
                for v in range(v0, nv):
                    f = c[k][v - v0]
                    if v == v0:
                        if k == 7:
                            continue
                        f = jnp.where(row8 > k, f, 0.0)
                    for kk in range(k + 1, 8):
                        c[kk][v - v0] = c[kk][v - v0] - f * scal[kk - k - 1]
                    ra[m][v] = ra[m][v] - f * row
                    rm[m][v] = rm[m][v] - f * mrow
    for m in range(4):
        ls, ms = [], []
        for v in range(nv):
            on = lane8 - row8 - (lo + 8 * v)
            d = jnp.sum(jnp.where(on == 0, ra[m][v], 0.0), axis=1, keepdims=True)
            s = lax.rsqrt(d)
            s = s * (1.5 - 0.5 * d * s * s)
            ls.append(jnp.where(on >= 0, ra[m][v] * s, 0.0))
            ms.append(rm[m][v] * s)
        ls = jnp.concatenate(ls, axis=0)
        ms = jnp.concatenate(ms, axis=0)
        mi[m, lo : lo + PB, :] = ms
        lt = ls.T
        fac[m, :, lo : lo + PB] = lt
        if lo + PB < B:
            g = jnp.dot(
                lt[lo + PB :, :],
                jnp.concatenate([ls, ms], axis=1),
                precision=HIGHEST,
                preferred_element_type=F32,
            )
            am[m, lo + PB :, :] -= g[:, :B]
            mi[m, lo + PB :, :] -= g[:, B:]


def window_kernel(
    pat_h, piv, low, pan_h, dia_h, out_h, fac_h,
    pat, ag, bg, bh, bl, lh, ll, part, sd, su, upd, ds, dsd, dsu, sb, pan, am, mi, fac, out,
    l_ss, a_ss, a_rs, af_ss, b_ss, b_rs, r_ss, rd_rs, ru_rs, d_ss, dd_rs, du_rs,
    s1_ss, s1_rs, s2_ss, s2_rs, y_ss, y_rs,
):
    c_me = lax.axis_index("col")
    r_me = lax.axis_index("row")
    z, h = c_me // 2, c_me % 2
    x, y = r_me // 4, r_me % 4
    oh = 1 - h
    xp, xm, xo = (x + 1) % 4, (x + 3) % 4, (x + 2) % 4
    yp, ym, yo = (y + 1) % 4, (y + 3) % 4, (y + 2) % 4
    zp, zm = (z + 1) % 8, (z + 7) % 8
    yh = y // 2

    own = [
        pltpu.make_async_copy(piv.at[pl.ds(NR * h, NR)], ag.at[:, x, h], l_ss.at[0]),
        pltpu.make_async_copy(pat_h, pat, l_ss.at[1]),
        pltpu.make_async_copy(low, bg.at[y, h], l_ss.at[2]),
        pltpu.make_async_copy(dia_h, am, l_ss.at[3]),
        pltpu.make_async_copy(pan_h, pan, l_ss.at[4]),
    ]
    for c in own:
        c.start()

    def dev(zz, hh, xx, yy):
        return (2 * zz + hh, 4 * xx + yy)

    def rcopy(src, dst, ss, rs, to):
        return pltpu.make_async_remote_copy(
            src_ref=src, dst_ref=dst, send_sem=ss, recv_sem=rs, device_id=to, device_id_type=MESH
        )

    here = dev(z, oh, x, y)

    def arrived(slot, ss, rs):
        rcopy(slot, slot, ss, rs, here).wait_recv()

    peers = [here, dev(zp, h, x, y), dev(zm, h, x, y)]
    for hh in (h, oh):
        peers += [dev(z, hh, xx, y) for xx in (xp, xm, xo)]
        peers += [dev(z, hh, x, yy) for yy in (yp, ym, yo)]
    bar = pltpu.get_barrier_semaphore()
    for p in peers:
        pl.semaphore_signal(bar, inc=1, device_id=p, device_id_type=MESH)
    pl.semaphore_wait(bar, len(peers))

    def rows(hh, i):
        return pl.ds(pl.multiple_of(2 * B * hh + RB * i, RB), RB)

    pending = []

    def go(c):
        c.start()
        pending.append(c)

    def send_a(i):
        for n, hh in enumerate((h, oh)):
            src = piv.at[NR * hh + i]
            go(rcopy(src, ag.at[i, x, h], a_ss.at[i, 2 * n], a_rs.at[i, 1, h], dev(z, hh, xp, y)))
            go(rcopy(src, ag.at[i, x, h], a_ss.at[i, 1 + 2 * n], a_rs.at[i, 2, h], dev(z, hh, xm, y)))

    go(rcopy(piv.at[pl.ds(NR * oh, NR)], ag.at[:, x, h], b_ss.at[9], b_rs.at[9], here))
    go(rcopy(low, bg.at[y, h], b_ss.at[1], b_rs.at[1], dev(z, h, x, yp)))
    go(rcopy(low, bg.at[y, h], b_ss.at[2], b_rs.at[2], dev(z, h, x, ym)))
    send_a(0)
    go(rcopy(low, bg.at[y, h], b_ss.at[0], b_rs.at[0], here))

    def weight(xr, i, kap, kb):
        return pat[2 * (2 * z + kap) + kb, 4 * (4 * xr + y) + 2 * h + i // 2].astype(F32)

    own[0].wait()
    own[1].wait()
    arrived(ag.at[:, x, oh], b_ss.at[9], b_rs.at[9])
    for t in range(2):
        m = jnp.concatenate(
            [
                jnp.concatenate(
                    [
                        ag[i, x, kap, :, kb * B : (kb + 1) * B] * weight(x, i, kap, kb)
                        for kap in range(2)
                        for kb in range(2)
                    ],
                    axis=1,
                )
                for i in (2 * t, 2 * t + 1)
            ],
            axis=0,
        )
        ds[t] = lax.dot_general(
            m, m, (((1,), (1,)), ((), ())), precision=HIGHEST, preferred_element_type=F32
        )

    d0 = (z - 2 * x - yh + 8) % 8

    def takes_down(d, s):
        return (d <= 3) if s == 0 else (d <= 2)

    def takes_up(d, s):
        return (d >= 6) | (d == 0) if s == 0 else (d >= 5) | (d == 0)

    def gives_down(d, s):
        return (d >= 1) & (d <= 4) if s == 0 else (d >= 1) & (d <= 3)

    def gives_up(d, s):
        return (d >= 5) if s == 0 else (d >= 4)

    def dsum_step(t, u, leaf):
        at = pl.ds(RB * u, RB)
        k = 2 * t + u
        tk_d, tk_u = takes_down(d0, t), takes_up(d0, t)
        if not leaf:

            @pl.when(tk_d)
            def _():
                arrived(dsd.at[t, at], d_ss.at[k], dd_rs.at[k])
                ds[t, at, :] += dsd[t, at, :]

            @pl.when(tk_u)
            def _():
                arrived(dsu.at[t, at], d_ss.at[k], du_rs.at[k])
                ds[t, at, :] += dsu[t, at, :]

        first = jnp.logical_not(tk_d | tk_u)
        turn = first if leaf else jnp.logical_not(first)

        @pl.when(turn & gives_down(d0, t))
        def _():
            rcopy(ds.at[t, at], dsd.at[t, at], d_ss.at[k], dd_rs.at[k], dev(zm, h, x, y)).start()

        @pl.when(turn & gives_up(d0, t))
        def _():
            rcopy(ds.at[t, at], dsu.at[t, at], d_ss.at[k], du_rs.at[k], dev(zp, h, x, y)).start()

    def forward_b():
        arrived(bg.at[ym, h], b_ss.at[1], b_rs.at[1])
        go(rcopy(bg.at[ym, h, 0:B], bg.at[ym, h, 0:B], b_ss.at[3], b_rs.at[3], dev(z, h, x, yp)))
        go(rcopy(bg.at[ym, h], bg.at[ym, h], b_ss.at[5], b_rs.at[5], here))
        arrived(bg.at[yp, h], b_ss.at[2], b_rs.at[2])
        go(rcopy(bg.at[yp, h, B:], bg.at[yp, h, B:], b_ss.at[4], b_rs.at[4], dev(z, h, x, ym)))
        go(rcopy(bg.at[yp, h], bg.at[yp, h], b_ss.at[6], b_rs.at[6], here))

    def forward_b2():
        arrived(bg.at[yo, h, 0:B], b_ss.at[3], b_rs.at[3])
        go(rcopy(bg.at[yo, h, 0:B], bg.at[yo, h, 0:B], b_ss.at[7], b_rs.at[7], here))
        arrived(bg.at[yo, h, B:], b_ss.at[4], b_rs.at[4])
        go(rcopy(bg.at[yo, h, B:], bg.at[yo, h, B:], b_ss.at[8], b_rs.at[8], here))

    def build_b():
        own[2].wait()
        arrived(bg.at[y, oh], b_ss.at[0], b_rs.at[0])
        arrived(bg.at[ym, oh], b_ss.at[5], b_rs.at[5])
        arrived(bg.at[yp, oh], b_ss.at[6], b_rs.at[6])
        arrived(bg.at[yo, oh, 0:B], b_ss.at[7], b_rs.at[7])
        arrived(bg.at[yo, oh, B:], b_ss.at[8], b_rs.at[8])
        for yy in range(4):
            for kap in range(2):
                hi, lo = split(bg[yy, kap])
                bh[kap * 256 : kap * 256 + 256, yy * B : yy * B + B] = hi
                bl[kap * 256 : kap * 256 + 256, yy * B : yy * B + B] = lo

    def forward_a(i):
        arrived(ag.at[i, xm, 0], a_ss.at[i, 0], a_rs.at[i, 1, 0])
        go(rcopy(ag.at[i, xm, 0], ag.at[i, xm, 0], af_ss.at[i, 0], a_rs.at[i, 3, 0], dev(z, h, xp, y)))
        arrived(ag.at[i, xp, 1], a_ss.at[i, 0], a_rs.at[i, 2, 1])
        go(rcopy(ag.at[i, xp, 1], ag.at[i, xp, 1], af_ss.at[i, 1], a_rs.at[i, 3, 1], dev(z, h, xm, y)))

    def product(i):
        arrived(ag.at[i, xm, 1], a_ss.at[i, 0], a_rs.at[i, 1, 1])
        arrived(ag.at[i, xp, 0], a_ss.at[i, 0], a_rs.at[i, 2, 0])
        arrived(ag.at[i, xo, 0], a_ss.at[i, 0], a_rs.at[i, 3, 0])
        arrived(ag.at[i, xo, 1], a_ss.at[i, 0], a_rs.at[i, 3, 1])
        for xr in range(4):
            for kap in range(2):
                for kb in range(2):
                    v = ag[i, xr, kap, :, kb * B : (kb + 1) * B] * weight(xr, i, kap, kb)
                    hi, lo = split(v)
                    k = (2 * kap + kb) * B
                    lh[xr * RB : xr * RB + RB, k : k + B] = hi
                    ll[xr * RB : xr * RB + RB, k : k + B] = lo
        p = jnp.dot(lh[...], bh[...], preferred_element_type=F32)
        p += jnp.dot(ll[...], bh[...], preferred_element_type=F32)
        p += jnp.dot(lh[...], bl[...], preferred_element_type=F32)
        for xr in range(4):
            part[i, xr] = p[xr * RB : xr * RB + RB]

    par = (z + yh) % 2
    odd, even = par == 1, par == 0
    e = (z - yh + 8) % 8
    offs = [jnp.where(even, ev, od) for ev, od in ((4, 3), (2, 5), (6, 1), (0, 7))]
    blks = [((e - d + 8) // 2) % 4 for d in offs]

    def reduce_step(i, q, s, leaf):
        d, xr = offs[q], blks[q]
        at = pl.ds(256 * s, 256)
        mine = part.at[i, xr, :, at]
        ss = r_ss.at[i, q, s]
        tk_d, tk_u = takes_down(d, s), takes_up(d, s)
        if not leaf:

            @pl.when(tk_d)
            def _():
                arrived(sd.at[i, xr, s], ss, rd_rs.at[i, xr, s])
                part[i, xr, :, at] += sd[i, xr, s]

            @pl.when(tk_u)
            def _():
                arrived(su.at[i, xr, s], ss, ru_rs.at[i, xr, s])
                part[i, xr, :, at] += su[i, xr, s]

        first = jnp.logical_not(tk_d | tk_u)
        turn = first if leaf else jnp.logical_not(first)

        @pl.when(turn & gives_down(d, s))
        def _():
            rcopy(mine, sd.at[i, xr, s], ss, rd_rs.at[i, xr, s], dev(zm, h, x, y)).start()

        @pl.when(turn & gives_up(d, s))
        def _():
            rcopy(mine, su.at[i, xr, s], ss, ru_rs.at[i, xr, s], dev(zp, h, x, y)).start()

    c_to = y % 2

    def leaves(i):
        for q in range(2):
            for s in range(2):
                reduce_step(i, q, s, True)

    def stage1(i):
        reduce_step(i, 0, 0, False)
        reduce_step(i, 1, 1, False)

    def stage2(i):
        reduce_step(i, 1, 1, False)
        reduce_step(i, 2, 0, False)
        reduce_step(i, 1, 0, False)
        reduce_step(i, 2, 1, False)

    def stage3(i):
        reduce_step(i, 2, 1, False)
        reduce_step(i, 3, 0, False)
        reduce_step(i, 2, 0, False)
        reduce_step(i, 3, 1, False)

    def stage4(i):
        for s in range(2):
            reduce_step(i, 3, s, False)
            for yy in (2 * s, 2 * s + 1):
                same = (yy == y) & (h == c_to)
                src = part.at[i, blks[3], :, pl.ds(B * yy, B)]

                @pl.when(same)
                def _():
                    upd[rows(h, i), :] = part[i, blks[3], :, pl.ds(B * yy, B)]

                @pl.when(jnp.logical_not(same))
                def _():
                    rcopy(
                        src, upd.at[rows(h, i)], y_ss.at[i, yy], y_rs.at[i, h], dev(z, c_to, x, yy)
                    ).start()

    root = d0 == 0
    relay = even & (h == c_to)

    def sum_x():
        @pl.when(root)
        def _():
            for t in range(2):
                for n, xx in enumerate((xp, xm, xo)):
                    rcopy(
                        ds.at[t], sb.at[2 * h + t], s1_ss.at[t, n], s1_rs.at[2 * h + t], dev(z, c_to, xx, y)
                    ).start()

                @pl.when(h != c_to)
                def _():
                    rcopy(ds.at[t], sb.at[2 * h + t], s1_ss.at[t, 3], s1_rs.at[2 * h + t], here).start()

                @pl.when(h == c_to)
                def _():
                    sb[2 * h + t] = ds[t]

    def sum_y():
        @pl.when(relay)
        def _():
            for t in range(4):
                @pl.when(jnp.logical_not(root & (h == t // 2)))
                def _():
                    arrived(sb.at[t], s1_ss.at[0, 0], s1_rs.at[t])

                for n, yy in enumerate((yp, ym, yo)):
                    rcopy(sb.at[t], sb.at[t], s2_ss.at[t, n], s2_rs.at[t], dev(z, h, x, yy)).start()

    def start_factor():
        own[3].wait()

        @pl.when(jnp.logical_not(relay))
        def _():
            for t in range(4):
                arrived(sb.at[t], s2_ss.at[t, 0], s2_rs.at[t])

        am[...] = am[...] - sb[...]
        eye = (
            lax.broadcasted_iota(jnp.int32, (B, B), 0) == lax.broadcasted_iota(jnp.int32, (B, B), 1)
        ).astype(F32)
        for m in range(4):
            mi[m] = eye

    near = (d0 <= 1) | (d0 == 7)
    pieces = [(t, u) for t in range(2) for u in range(2)]

    def chain():
        for t, u in pieces:
            dsum_step(t, u, False)

    def on_odd(*steps):
        @pl.when(odd)
        def _():
            for f, i in steps:
                f(i)

    def on_even(*steps):
        @pl.when(even)
        def _():
            for f, i in steps:
                f(i)

    for t, u in pieces:
        dsum_step(t, u, True)
    send_a(1)
    forward_a(0)
    forward_b()
    send_a(2)
    pl.when(jnp.logical_not(near))(chain)
    forward_b2()
    build_b()
    product(0)
    leaves(0)
    forward_a(1)
    send_a(3)

    @pl.when(near)
    def _():
        chain()
        sum_x()

    for i in range(NR):
        if i > 0:
            product(i)
            leaves(i)
            if i + 1 < NR:
                forward_a(i + 1)
        if i == 2:
            sum_y()
        on_odd(*([(stage1, i)] + ([(stage3, i - 1)] if i >= 1 else [])))
        on_even(*(([(stage2, i - 1)] if i >= 1 else []) + ([(stage4, i - 2)] if i >= 2 else [])))
    on_even((stage2, 3))
    start_factor()
    factor_panel(0, am, mi, fac)
    on_odd((stage3, 3))
    on_even((stage4, 2))
    factor_panel(1, am, mi, fac)
    factor_panel(2, am, mi, fac)
    on_even((stage4, 3))
    factor_panel(3, am, mi, fac)
    fac_out = pltpu.make_async_copy(fac, fac_h, l_ss.at[5])
    fac_out.start()

    own[4].wait()
    y_src = 2 * (z % 2) + h
    for i in range(NR):
        for hh in range(2):

            @pl.when(jnp.logical_not((y == y_src) & (h == hh)))
            def _():
                arrived(upd.at[rows(hh, i)], y_ss.at[i, 0], y_rs.at[i, hh])

    for m in range(4):
        at = slice(m * B, m * B + B)
        out[at, :] = jnp.dot(
            mi[m], pan[at, :] - upd[at, :], precision=HIGHEST, preferred_element_type=F32
        )
    panel_out = pltpu.make_async_copy(out, out_h, l_ss.at[6])
    panel_out.start()

    for c in pending:
        c.wait_send()
    for t, u in pieces:
        k = 2 * t + u
        at = pl.ds(RB * u, RB)

        @pl.when(jnp.logical_not(root))
        def _():
            rcopy(ds.at[t, at], dsd.at[t, at], d_ss.at[k], dd_rs.at[k], here).wait_send()

    for i in range(NR):
        for q in range(4):
            for s in range(2):

                @pl.when(offs[q] != 0)
                def _():
                    rcopy(
                        part.at[i, blks[q], :, pl.ds(256 * s, 256)], sd.at[i, blks[q], s],
                        r_ss.at[i, q, s], rd_rs.at[i, blks[q], s], here,
                    ).wait_send()

        @pl.when(even)
        def _():
            for yy in range(4):
                @pl.when(jnp.logical_not((yy == y) & (h == c_to)))
                def _():
                    rcopy(
                        part.at[i, blks[3], :, pl.ds(B * yy, B)], upd.at[rows(h, i)],
                        y_ss.at[i, yy], y_rs.at[i, h], here,
                    ).wait_send()

    @pl.when(root)
    def _():
        for t in range(2):
            for n in range(3):
                rcopy(ds.at[t], sb.at[t], s1_ss.at[t, n], s1_rs.at[t], here).wait_send()

            @pl.when(h != c_to)
            def _():
                rcopy(ds.at[t], sb.at[t], s1_ss.at[t, 3], s1_rs.at[t], here).wait_send()

    @pl.when(relay)
    def _():
        for t in range(4):
            for n in range(3):
                rcopy(sb.at[t], sb.at[t], s2_ss.at[t, n], s2_rs.at[t], here).wait_send()

    fac_out.wait()
    panel_out.wait()


def window(pattern, pivot_rows, lower_cols, panel_in, diag_in):
    anyspace = pl.BlockSpec(memory_space=pltpu.HBM)
    dma = pltpu.SemaphoreType.DMA
    return pl.pallas_call(
        window_kernel,
        out_shape=(
            jax.ShapeDtypeStruct((4 * B, B), F32),
            jax.ShapeDtypeStruct((4, B, B), F32),
        ),
        in_specs=[anyspace] * 5,
        out_specs=(anyspace, anyspace),
        scratch_shapes=[
            pltpu.SMEM((32, 64), jnp.int32),
            pltpu.VMEM((NR, 4, 2, RB, 256), F32),
            pltpu.VMEM((4, 2, 256, B), F32),
            pltpu.VMEM((512, 512), BF16),
            pltpu.VMEM((512, 512), BF16),
            pltpu.VMEM((4 * RB, 512), BF16),
            pltpu.VMEM((4 * RB, 512), BF16),
            pltpu.VMEM((NR, 4, RB, 512), F32),
            pltpu.VMEM((NR, 4, 2, RB, 256), F32),
            pltpu.VMEM((NR, 4, 2, RB, 256), F32),
            pltpu.VMEM((4 * B, B), F32),
            pltpu.VMEM((2, B, B), F32),
            pltpu.VMEM((2, B, B), F32),
            pltpu.VMEM((2, B, B), F32),
            pltpu.VMEM((4, B, B), F32),
            pltpu.VMEM((4 * B, B), F32),
            pltpu.VMEM((4, B, B), F32),
            pltpu.VMEM((4, B, B), F32),
            pltpu.VMEM((4, B, B), F32),
            pltpu.VMEM((4 * B, B), F32),
            dma((7,)), dma((NR, 4)), dma((NR, 4, 2)), dma((NR, 2)), dma((10,)), dma((10,)),
            dma((NR, 4, 2)), dma((NR, 4, 2)), dma((NR, 4, 2)), dma((4,)), dma((4,)), dma((4,)),
            dma((2, 4)), dma((4,)), dma((4, 3)), dma((4,)), dma((NR, 4)), dma((NR, 2)),
        ],
        compiler_params=pltpu.CompilerParams(
            collective_id=0, has_side_effects=True, vmem_limit_bytes=60 << 20
        ),
        name="window",
    )(pattern.T, pivot_rows.reshape(2 * NR, RB, 256), lower_cols, panel_in, diag_in)


def shards(lower_cols, pivot_rows, pattern, panel_in, diag_in):
    return window(pattern, pivot_rows, lower_cols, panel_in, diag_in)


def solution(mesh):
    in_specs = (P("col", "row"), P("row", "col"), P(), P("col", "row"), P("col", None, None))
    out_specs = (P("col", "row"), P("col", None, None))
    return jax.shard_map(shards, mesh=mesh, in_specs=in_specs, out_specs=out_specs, check_vma=False)
```
